32 devices in a mesh: grp: 4 (over z), ctx: 8 (over y, x, core).
Axes of the slice: x: 2, y: 2, z: 4, core: 2. Of those that a mesh axis runs over, the one named last changes fastest.
Arguments:
- query_rows: bfloat16 [32768, 512], P(('grp', 'ctx')), may hold values from -6 to 6
- key_rows: bfloat16 [32768, 512], P(('grp', 'ctx')), may hold values from -6 to 6
- value_rows: bfloat16 [32768, 512], P(('grp', 'ctx')), may hold values from -6 to 6
- cluster_ids: int32 [4, 32768], P(None, ('grp', 'ctx')), may hold values from 0 to 255, as said below
Outputs:
- attended: bfloat16 [32768, 512], P(('grp', 'ctx'))
The draws below stay inside these ranges and needn't reach their ends.
Inputs may be any that keep to these rules, and one draw needn't show every extreme that they name: `cluster_ids`: for each head, the tokens of one device whose clusters share one value of id // 8 number at most 96; for each head one such range receives exactly 96 tokens from every device, and every other range at most 32 from one device. For each head and range, the sum over its clusters of their token counts rounded up to multiples of 128 is at most 3072, with equality for the range that is full.
All inputs are finite; a program needn't handle non-finite values.
Results may differ from the reference program's by a relative error of at most 0.0034.
Values may be sent and summed in bfloat16 or wider, within the bound.
A program may use at most 128 MiB of HBM per device.

```python
import jax
import jax.numpy as jnp
from jax import lax

HEADS = 4
HD = 128
CL_DEV = 8
TILE = 128
TOK_DEV = 1024
TOKENS = 32768


def routing_plan(key):
    device_count = TOKENS // TOK_DEV
    capacity = 3 * TOK_DEV // device_count
    modest = TOK_DEV // device_count
    busy_rows = device_count * capacity
    tile_count = busy_rows // TILE
    pool_size = (device_count - 1) * modest
    root_key = jax.random.fold_in(key, 7101)
    label_list = []
    busiest_list = []
    for head_pos in range(HEADS):
        head_key = jax.random.fold_in(root_key, head_pos)
        busiest = jax.random.randint(jax.random.fold_in(head_key, 1), (), 0, device_count).astype(jnp.int32)
        pick_keys = jax.random.split(jax.random.fold_in(head_key, 2), device_count)
        picked = jax.vmap(lambda one_key: jax.random.permutation(one_key, pool_size)[:TOK_DEV - capacity])(pick_keys)
        others = (picked // modest).astype(jnp.int32)
        others = others + (others >= busiest).astype(jnp.int32)
        targets = jnp.concatenate([jnp.full((device_count, capacity), busiest, jnp.int32), others], axis=1)
        order_keys = jax.random.split(jax.random.fold_in(head_key, 3), device_count)
        targets = jax.vmap(lambda one_key, one_row: jax.random.permutation(one_key, one_row))(order_keys, targets)
        first_pick = jax.random.randint(jax.random.fold_in(head_key, 4), (device_count, TOK_DEV), 0, CL_DEV)
        second_pick = jax.random.randint(jax.random.fold_in(head_key, 5), (device_count, TOK_DEV), 0, CL_DEV)
        spread = jnp.minimum(first_pick, second_pick).astype(jnp.int32)
        cut_points = jnp.sort(jax.random.permutation(jax.random.fold_in(head_key, 6), tile_count - 1)[:CL_DEV - 1] + 1)
        row_index = jnp.arange(busy_rows, dtype=jnp.int32)
        busy_labels = jnp.sum((row_index[:, None] >= cut_points[None, :] * TILE).astype(jnp.int32), axis=1)
        busy_labels = jax.random.permutation(jax.random.fold_in(head_key, 7), busy_labels)
        at_busiest = (targets == busiest).astype(jnp.int32)
        busy_rank = jnp.cumsum(at_busiest, axis=1) - at_busiest
        source_index = jnp.arange(device_count, dtype=jnp.int32)[:, None]
        lookup = jnp.minimum(source_index * capacity + busy_rank, busy_rows - 1)
        local_ids = jnp.where(at_busiest == 1, busy_labels[lookup], spread)
        label_list.append((targets * CL_DEV + local_ids).reshape(-1).astype(jnp.int32))
        busiest_list.append(busiest)
    return jnp.stack(label_list, axis=0)


def draw_cluster_ids(key, part):
    return routing_plan(key)


def drawn(key, which):
    noise_key = jax.random.fold_in(key, 9300 + which)
    values = jnp.clip(jax.random.normal(noise_key, (TOKENS, HEADS, HD), jnp.float32), -6.0, 6.0)
    return values.reshape(TOKENS, HEADS * HD).astype(jnp.bfloat16)


def draw_query_rows(key, part):
    return drawn(key, 0)


def draw_key_rows(key, part):
    return drawn(key, 1)


def shard_levels(rng, dims, cuts, smallest, top_value):
    def one(position, parts):
        heights = jax.random.uniform(jax.random.fold_in(jax.random.fold_in(rng, 6), position), (parts,), jnp.float32, smallest / len(cuts), top_value / len(cuts))
        return jnp.repeat(jnp.exp(heights), dims[position] // parts).reshape((-1,) + (1,) * (len(dims) - position - 1))

    factor_of = one(*cuts[0])
    for cut in cuts[1:]:
        factor_of = factor_of * one(*cut)
    return factor_of


def centred(own_key, shape, width, bound, cuts=(), kind=jnp.bfloat16):
    array = jax.random.normal(own_key, shape, jnp.float32) * width
    if len(cuts) > 0:
        array = shard_levels(own_key, shape, cuts, -0.22, 0.18) * array
    return jnp.clip(array, min=-bound, max=bound).astype(kind)


def setup_inputs(seed: int = 0) -> dict:
    seeds = jax.random.split(jax.random.key(seed), 5)
    query_rows = draw_query_rows(jax.random.fold_in(seeds[4], 71), 0)
    key_rows = draw_key_rows(jax.random.fold_in(seeds[4], 71), 0)
    value_rows = centred(seeds[2], (TOKENS, HEADS * HD), 1.0, 6.0, ((0, 32),))
    cluster_ids = draw_cluster_ids(jax.random.fold_in(seeds[4], 71), 0)
    return {"query_rows": query_rows, "key_rows": key_rows, "value_rows": value_rows, "cluster_ids": cluster_ids}


NEG_FILL = -1.0e30


def head_output(query_head, key_head, value_head, labels):
    total_rows = query_head.shape[0]
    positions = jnp.arange(total_rows, dtype=jnp.int32)
    sort_order = jnp.argsort(labels * total_rows + positions).astype(jnp.int32)
    sorted_query = query_head[sort_order]
    sorted_key = key_head[sort_order]
    sorted_value = value_head[sort_order]
    sorted_label = labels[sort_order]
    previous = jnp.concatenate([jnp.full((1,), -1, jnp.int32), sorted_label[:-1]])
    region_start = lax.cummax(jnp.where(sorted_label != previous, positions, 0), axis=0)
    block_rows = 256
    first_rows = region_start.reshape(-1, block_rows)[:, 0]
    score_scale = HD ** -0.5

    def one_block(block_index):
        row_start = block_index * block_rows
        query_part = lax.dynamic_slice_in_dim(sorted_query, row_start, block_rows, 0)
        query_label = lax.dynamic_slice_in_dim(sorted_label, row_start, block_rows, 0)
        query_pos = row_start + jnp.arange(block_rows, dtype=jnp.int32)

        def key_block(key_index, state_now):
            run_max, run_sum, weighted = state_now
            key_start = key_index * block_rows
            key_part = lax.dynamic_slice_in_dim(sorted_key, key_start, block_rows, 0)
            value_part = lax.dynamic_slice_in_dim(sorted_value, key_start, block_rows, 0)
            key_label = lax.dynamic_slice_in_dim(sorted_label, key_start, block_rows, 0)
            key_pos = key_start + jnp.arange(block_rows, dtype=jnp.int32)
            scores = jnp.dot(query_part, key_part.T, preferred_element_type=jnp.float32) * score_scale
            allowed = (query_label[:, None] == key_label[None, :]) & (key_pos[None, :] <= query_pos[:, None])
            masked = jnp.where(allowed, scores, NEG_FILL)
            new_max = jnp.maximum(run_max, jnp.max(masked, axis=1))
            weights = jnp.where(allowed, jnp.exp(masked - new_max[:, None]), 0.0)
            factor = jnp.exp(run_max - new_max)
            run_sum = run_sum * factor + jnp.sum(weights, axis=1)
            weighted = weighted * factor[:, None] + jnp.dot(weights.astype(jnp.bfloat16), value_part, preferred_element_type=jnp.float32)
            return new_max, run_sum, weighted

        start_state = (jnp.full((block_rows,), NEG_FILL, jnp.float32), jnp.zeros((block_rows,), jnp.float32), jnp.zeros((block_rows, HD), jnp.float32))
        first_block = first_rows[block_index] // block_rows
        run_max, run_sum, weighted = lax.fori_loop(first_block, block_index + 1, key_block, start_state)
        return (weighted / run_sum[:, None]).astype(jnp.bfloat16)

    block_ids = jnp.arange(total_rows // block_rows, dtype=jnp.int32)
    sorted_out = lax.map(one_block, block_ids).reshape(total_rows, HD)
    return jnp.zeros_like(sorted_out).at[sort_order].set(sorted_out)


def reference(query_rows, key_rows, value_rows, cluster_ids):
    query_split = query_rows.reshape(TOKENS, HEADS, HD)
    key_split = key_rows.reshape(TOKENS, HEADS, HD)
    value_split = value_rows.reshape(TOKENS, HEADS, HD)
    outputs = []
    for head_pos in range(HEADS):
        outputs.append(head_output(query_split[:, head_pos], key_split[:, head_pos], value_split[:, head_pos], cluster_ids[head_pos]))
    return jnp.stack(outputs, axis=1).reshape(TOKENS, HEADS * HD)
```

```python
import functools
import math

import jax
import jax.numpy as jnp
from jax import lax
from jax.experimental import pallas as pl
from jax.experimental.pallas import tpu as pltpu
from jax.sharding import PartitionSpec as P

CL_SHIFT = 3
LANES = 128
SUB = 16
NEG_FILL = -1e30
F32 = jnp.float32
BF16 = jnp.bfloat16


def up(value, step):
    return (value + step - 1) // step * step


class Plan:
    def __init__(self, devices, heads, tokens):
        self.devices, self.heads, self.tokens = devices, heads, tokens
        self.cap = tokens // devices
        self.busy = 3 * tokens // devices
        self.stride = up(self.cap, SUB)
        self.bstride = up(self.busy, SUB)
        self.servers = devices // heads
        self.share = -(-self.busy // self.servers)
        self.base = devices * self.stride
        self.qstride = up(self.share, SUB)
        self.extra = self.servers * self.qstride
        self.row_k = heads * 3 * self.stride
        self.row_v = self.row_k + self.bstride
        self.row_q = self.row_v + self.bstride
        self.row_l = self.row_q + self.qstride
        self.rows = self.row_l + SUB
        self.ans_q = heads * self.stride
        self.ans_rows = self.ans_q + self.qstride


def iota(shape, dim):
    return lax.broadcasted_iota(jnp.int32, shape, dim)


def dot(a, b):
    return jnp.dot(a, b, preferred_element_type=F32)


def dot_t(a, b):
    return lax.dot_general(a, b, (((1,), (1,)), ((), ())), preferred_element_type=F32)


def onehot(cond):
    return jnp.where(cond, 1.0, 0.0).astype(BF16)


def shift_of(value):
    assert value & (value - 1) == 0
    return value.bit_length() - 1


def pack(p, ids_ref, q_ref, k_ref, v_ref, send_ref, key_ref):
    n, t = p.devices, p.tokens
    earlier = onehot(iota((t, t), 0) < iota((t, t), 1))
    label_sum = jnp.zeros((n, LANES), F32)
    busy_sum = jnp.zeros((n, LANES), F32)
    for h in range(p.heads):
        ids = ids_ref[h : h + 1, :]
        owner = lax.shift_right_logical(ids, CL_SHIFT)
        label = ((ids & (2**CL_SHIFT - 1)) + 1).astype(F32)
        member = jnp.where(iota((n, t), 0) == owner, 1.0, 0.0)
        rank = dot(member.astype(BF16), earlier)
        slot = jnp.sum(member * rank, axis=0, keepdims=True)
        full = jnp.where(jnp.sum(member, axis=1, keepdims=True) > p.cap, 1.0, 0.0)
        is_busy = jnp.sum(member * full, axis=0, keepdims=True) > 0.5
        share_pos = jnp.floor((slot + 0.5) * (1.0 / p.share))
        key_ref[h : h + 1, :] = jnp.where(
            is_busy,
            p.base + slot + share_pos * (p.qstride - p.share),
            owner.astype(F32) * p.stride + slot,
        )
        slot_i = slot.astype(jnp.int32)
        key = jnp.where(is_busy, -1, owner * p.stride + slot_i)
        rank_busy = jnp.where(is_busy, slot_i, -1)
        place = jnp.where(is_busy, -1, h * p.stride + slot_i)
        columns = pl.ds(h * LANES, LANES)
        data = jnp.concatenate([q_ref[:, columns], k_ref[:, columns], v_ref[:, columns]], axis=1)
        select = onehot(iota((p.base, t), 0) == key)
        moved = dot(select, data).astype(BF16)
        for part in range(3):
            row = (3 * h + part) * p.stride
            send_ref[:, row : row + p.stride, :] = moved[
                :, part * LANES : (part + 1) * LANES
            ].reshape(n, p.stride, LANES)
        rows = iota((p.bstride, t), 0)
        moved = dot(onehot(rows == rank_busy), data[:, LANES:]).astype(BF16)
        for j in range(p.servers):
            target = h * p.servers + j
            send_ref[target, p.row_k : p.row_k + p.bstride, :] = moved[:, :LANES]
            send_ref[target, p.row_v : p.row_v + p.bstride, :] = moved[:, LANES:]
        rows = iota((p.extra, t), 0)
        within = rows & (p.qstride - 1)
        wanted = lax.shift_right_logical(rows, shift_of(p.qstride)) * p.share + within
        wanted = jnp.where(within < p.share, wanted, -2)
        moved = dot(onehot(wanted == rank_busy), data[:, :LANES]).astype(BF16)
        first = h * p.servers
        send_ref[first : first + p.servers, p.row_q : p.row_q + p.qstride, :] = moved.reshape(
            p.servers, p.qstride, LANES
        )
        spot = onehot(iota((LANES, t), 0) == place)
        label_sum += dot_t((member * label).astype(BF16), spot)
        spot = onehot(iota((LANES, t), 0) == rank_busy)
        line = dot_t(jnp.broadcast_to(label, (8, t)).astype(BF16), spot)[:1]
        mine = lax.shift_right_logical(iota((n, LANES), 0), shift_of(p.servers)) == h
        busy_sum += jnp.where(mine, jnp.broadcast_to(line, (n, LANES)), 0.0)
    rows, target = iota((n * SUB, n), 0), iota((n * SUB, n), 1)
    same = (rows >> shift_of(SUB)) == target
    lower = (rows & (SUB - 1)) < SUB // 2
    both = dot(onehot(same & lower), label_sum.astype(BF16)) + dot(
        onehot(same & jnp.logical_not(lower)), busy_sum.astype(BF16)
    )
    send_ref[:, p.row_l : p.row_l + SUB, :] = both.astype(BF16).reshape(n, SUB, LANES)


def softmax_rows(scores, allowed, values, factor):
    masked = jnp.where(allowed, scores, NEG_FILL)
    top = jnp.max(masked, axis=1, keepdims=True)
    weights = jnp.exp2((masked - top) * factor)
    total = jnp.sum(weights, axis=1, keepdims=True)
    return (dot(weights.astype(BF16), values) / total).astype(BF16)


def attend(p, me, recv_ref, ans_ref):
    n = p.devices
    factor = LANES**-0.5 * math.log2(math.e)
    label_block = recv_ref[:, p.row_l : p.row_l + SUB, :].reshape(n * SUB, LANES)
    pick = iota((n, n * SUB), 1) - iota((n, n * SUB), 0) * SUB
    labels = dot(onehot(pick == 0), label_block).astype(BF16)
    busy_labels = dot(onehot(pick == SUB // 2), label_block).astype(BF16)

    def lane_labels(table, width, offset):
        total = n * width
        lane = iota((n, total), 1)
        group = jnp.floor((iota((1, total), 1).astype(F32) + 0.5) * (1.0 / width)).astype(
            jnp.int32
        )
        within = iota((1, total), 1) - group * width
        spread = dot(table, onehot(iota((LANES, total), 0) == within + offset))
        return jnp.sum(jnp.where(iota((n, total), 0) == group, spread, 0.0), axis=0, keepdims=True)

    def row_labels(table, width, offset):
        total = n * width
        rows = iota((total, n), 0)
        shift = shift_of(width)
        spread = dot(onehot((rows >> shift) == iota((total, n), 1)), table)
        lane = (iota((total, LANES), 0) & (width - 1)) + offset
        return jnp.sum(
            jnp.where(iota((total, LANES), 1) == lane, spread, 0.0), axis=1, keepdims=True
        )

    block = math.gcd(n, max(1, 256 // p.stride))
    for h in range(p.heads):
        key_label = lane_labels(labels, p.stride, h * p.stride)
        query_label = row_labels(labels, p.stride, h * p.stride)
        row = 3 * h * p.stride
        for start in range(0, n, block):
            size, keys = block * p.stride, (start + block) * p.stride
            first = start * p.stride
            queries = recv_ref[start : start + block, row : row + p.stride, :]
            keys_part = recv_ref[: start + block, row + p.stride : row + 2 * p.stride, :]
            values = recv_ref[: start + block, row + 2 * p.stride : row + 3 * p.stride, :]
            scores = dot_t(queries.reshape(size, LANES), keys_part.reshape(keys, LANES))
            allowed = (query_label[first : first + size] == key_label[:, :keys]) & (
                iota((size, keys), 1) <= iota((size, keys), 0) + first
            )
            out = softmax_rows(scores, allowed, values.reshape(keys, LANES), factor)
            ans_ref[start : start + block, h * p.stride : (h + 1) * p.stride, :] = out.reshape(
                block, p.stride, LANES
            )
    share_first = lax.rem(me, p.servers) * p.share
    key_label = lane_labels(busy_labels, p.bstride, 0)
    query_label = row_labels(busy_labels, p.qstride, share_first)
    block = math.gcd(n, max(1, 128 // p.qstride))
    for start in range(0, n, block):
        size, keys = block * p.qstride, (start + block) * p.bstride
        first = start * p.qstride
        queries = recv_ref[start : start + block, p.row_q : p.row_q + p.qstride, :]
        keys_part = recv_ref[: start + block, p.row_k : p.row_k + p.bstride, :]
        values = recv_ref[: start + block, p.row_v : p.row_v + p.bstride, :]
        scores = dot_t(queries.reshape(size, LANES), keys_part.reshape(keys, LANES))
        rows = iota((size, 1), 0)
        place = (
            ((rows >> shift_of(p.qstride)) + start) * p.bstride
            + (rows & (p.qstride - 1))
            + share_first
        )
        allowed = (query_label[first : first + size] == key_label[:, :keys]) & (
            iota((size, keys), 1) <= place
        )
        out = softmax_rows(scores, allowed, values.reshape(keys, LANES), factor)
        ans_ref[start : start + block, p.ans_q : p.ans_q + p.qstride, :] = out.reshape(
            block, p.qstride, LANES
        )


def unpack(p, key_ref, back_ref, out_ref):
    n, t = p.devices, p.tokens
    keys = jnp.concatenate([key_ref[...]] + [jnp.zeros((8 - p.heads, t), F32)], axis=0)
    key_columns = jnp.transpose(keys).astype(jnp.int32)
    total = p.base + p.extra
    for h in range(p.heads):
        select = onehot(iota((t, total), 1) == key_columns[:, h : h + 1])
        rows = back_ref[:, h * p.stride : (h + 1) * p.stride, :].reshape(p.base, LANES)
        first = h * p.servers
        more = back_ref[first : first + p.servers, p.ans_q : p.ans_q + p.qstride, :]
        rows = jnp.concatenate([rows, more.reshape(p.extra, LANES)], axis=0)
        out_ref[:, h * LANES : (h + 1) * LANES] = dot(select, rows).astype(BF16)


VMEM_SPEC = pl.BlockSpec(memory_space=pltpu.VMEM)
PARAMS = dict(vmem_limit_bytes=56 * 2**20)


def local(query_rows, key_rows, value_rows, cluster_ids):
    axes = ("grp", "ctx")
    devices = lax.axis_size("grp") * lax.axis_size("ctx")
    heads, tokens = cluster_ids.shape
    p = Plan(devices, heads, tokens)

    def pack_kernel(*refs):
        pack(p, *refs)

    def attend_kernel(recv_ref, ans_ref):
        me = lax.axis_index("grp") * lax.axis_size("ctx") + lax.axis_index("ctx")
        attend(p, me, recv_ref, ans_ref)

    def unpack_kernel(*refs):
        unpack(p, *refs)

    send, keys = pl.pallas_call(
        pack_kernel,
        out_shape=(
            jax.ShapeDtypeStruct((devices, p.rows, LANES), BF16),
            jax.ShapeDtypeStruct((heads, tokens), F32),
        ),
        in_specs=[VMEM_SPEC] * 4,
        out_specs=(VMEM_SPEC, VMEM_SPEC),
        compiler_params=pltpu.CompilerParams(**PARAMS),
    )(cluster_ids, query_rows, key_rows, value_rows)
    recv = lax.all_to_all(send, axes, split_axis=0, concat_axis=0, tiled=True)
    ans = pl.pallas_call(
        attend_kernel,
        out_shape=jax.ShapeDtypeStruct((devices, p.ans_rows, LANES), BF16),
        in_specs=[VMEM_SPEC],
        out_specs=VMEM_SPEC,
        compiler_params=pltpu.CompilerParams(**PARAMS),
    )(recv)
    back = lax.all_to_all(ans, axes, split_axis=0, concat_axis=0, tiled=True)
    return pl.pallas_call(
        unpack_kernel,
        out_shape=jax.ShapeDtypeStruct((tokens, heads * LANES), BF16),
        in_specs=[VMEM_SPEC] * 2,
        out_specs=VMEM_SPEC,
        compiler_params=pltpu.CompilerParams(**PARAMS),
    )(keys, back)


def solution(mesh):
    return jax.shard_map(
        local,
        mesh=mesh,
        in_specs=(
            P(("grp", "ctx"), None),
            P(("grp", "ctx"), None),
            P(("grp", "ctx"), None),
            P(None, ("grp", "ctx")),
        ),
        out_specs=P(("grp", "ctx"), None),
        check_vma=False,
    )
```

```python
import functools
import math

import jax
import jax.numpy as jnp
from jax import lax
from jax.experimental import pallas as pl
from jax.experimental.pallas import tpu as pltpu
from jax.sharding import PartitionSpec as P

CL_SHIFT = 3
LANES = 128
SUB = 16
NEG_FILL = -1e30
F32 = jnp.float32
BF16 = jnp.bfloat16


def up(value, step):
    return (value + step - 1) // step * step


class Plan:
    def __init__(self, devices, heads, tokens):
        self.devices, self.heads, self.tokens = devices, heads, tokens
        self.cap = tokens // devices
        self.busy = 3 * tokens // devices
        self.stride = up(self.cap, SUB)
        self.per_head = devices // heads
        self.servers = min(self.per_head, max(1, self.busy // 12))
        self.share = -(-self.busy // self.servers)
        self.base = devices * self.stride
        self.qstride = up(self.share, SUB)
        self.extra = self.servers * self.qstride
        self.row_b = heads * 3 * self.stride
        self.row_q = self.row_b + 2 * self.qstride
        self.row_l = self.row_q + self.qstride
        self.rows = self.row_l + SUB
        self.ans_q = heads * self.stride
        self.ans_rows = self.ans_q + self.qstride
        self.chunks = [(self.row_b, self.rows - self.row_b)]
        self.chunks += [(3 * h * self.stride, 3 * self.stride) for h in range(heads)]
        self.ans_chunks = [(self.ans_q, self.qstride)]
        self.ans_chunks += [(h * self.stride, self.stride) for h in range(heads)]


def iota(shape, dim):
    return lax.broadcasted_iota(jnp.int32, shape, dim)


def dot(a, b):
    return jnp.dot(a, b, preferred_element_type=F32)


def dot_t(a, b):
    return lax.dot_general(a, b, (((1,), (1,)), ((), ())), preferred_element_type=F32)


def onehot(cond):
    return jnp.where(cond, 1.0, 0.0).astype(BF16)


def shift_of(value):
    assert value & (value - 1) == 0
    return value.bit_length() - 1


def pack_shared(p, ids_ref, q_ref, k_ref, v_ref, send_ref, key_ref, base_key_ref):
    n, t = p.devices, p.tokens
    earlier = onehot(iota((t, t), 0) < iota((t, t), 1))
    key_ref[...] = jnp.zeros(key_ref.shape, F32)
    label_sum = jnp.zeros((n, LANES), F32)
    busy_sum = jnp.zeros((n, LANES), F32)
    for h in range(p.heads):
        ids = ids_ref[h : h + 1, :]
        owner = lax.shift_right_logical(ids, CL_SHIFT)
        label = ((ids & (2**CL_SHIFT - 1)) + 1).astype(F32)
        member = jnp.where(iota((n, t), 0) == owner, 1.0, 0.0)
        rank = dot(member.astype(BF16), earlier)
        slot = jnp.sum(member * rank, axis=0, keepdims=True)
        full = jnp.where(jnp.sum(member, axis=1, keepdims=True) > p.cap, 1.0, 0.0)
        is_busy = jnp.sum(member * full, axis=0, keepdims=True) > 0.5
        share_pos = jnp.floor((slot + 0.5) * (1.0 / p.share))
        key_ref[h : h + 1, :] = jnp.where(
            is_busy,
            p.base + slot + share_pos * (p.qstride - p.share),
            owner.astype(F32) * p.stride + slot,
        )
        slot_i = slot.astype(jnp.int32)
        base_key_ref[h : h + 1, :] = jnp.where(is_busy, -1, owner * p.stride + slot_i)
        rank_busy = jnp.where(is_busy, slot_i, -1)
        place = jnp.where(is_busy, -1, h * p.stride + slot_i)
        columns = pl.ds(h * LANES, LANES)
        data = jnp.concatenate([k_ref[:, columns], v_ref[:, columns], q_ref[:, columns]], axis=1)
        rows = iota((p.extra, t), 0)
        within = rows & (p.qstride - 1)
        wanted = lax.shift_right_logical(rows, shift_of(p.qstride)) * p.share + within
        wanted = jnp.where(within < p.share, wanted, -2)
        moved = dot(onehot(wanted == rank_busy), data).astype(BF16)
        first = h * p.per_head
        for part in range(3):
            row = p.row_b + part * p.qstride
            send_ref[first : first + p.servers, row : row + p.qstride, :] = moved[
                :, part * LANES : (part + 1) * LANES
            ].reshape(p.servers, p.qstride, LANES)
        if p.servers < p.per_head:
            send_ref[
                first + p.servers : first + p.per_head, p.row_b : p.row_l, :
            ] = jnp.zeros((p.per_head - p.servers, 3 * p.qstride, LANES), BF16)
        spot = onehot(iota((LANES, t), 0) == place)
        label_sum += dot_t((member * label).astype(BF16), spot)
        spot = onehot(iota((LANES, t), 0) == rank_busy)
        line = dot_t(jnp.broadcast_to(label, (8, t)).astype(BF16), spot)[:1]
        mine = lax.shift_right_logical(iota((n, LANES), 0), shift_of(p.per_head)) == h
        busy_sum += jnp.where(mine, jnp.broadcast_to(line, (n, LANES)), 0.0)
    rows, target = iota((n * SUB, n), 0), iota((n * SUB, n), 1)
    same = (rows >> shift_of(SUB)) == target
    lower = (rows & (SUB - 1)) < SUB // 2
    both = dot(onehot(same & lower), label_sum.astype(BF16)) + dot(
        onehot(same & jnp.logical_not(lower)), busy_sum.astype(BF16)
    )
    send_ref[:, p.row_l : p.row_l + SUB, :] = both.astype(BF16).reshape(n, SUB, LANES)


def pack_head(p, h, q_ref, k_ref, v_ref, send_ref, base_key_ref):
    columns = pl.ds(h * LANES, LANES)
    data = jnp.concatenate([q_ref[:, columns], k_ref[:, columns], v_ref[:, columns]], axis=1)
    select = onehot(iota((p.base, p.tokens), 0) == base_key_ref[h : h + 1, :])
    moved = dot(select, data).astype(BF16)
    for part in range(3):
        row = (3 * h + part) * p.stride
        send_ref[:, row : row + p.stride, :] = moved[
            :, part * LANES : (part + 1) * LANES
        ].reshape(p.devices, p.stride, LANES)


def softmax_rows(scores, allowed, values, factor):
    masked = jnp.where(allowed, scores, NEG_FILL)
    top = jnp.max(masked, axis=1, keepdims=True)
    weights = jnp.exp2((masked - top) * factor)
    total = jnp.sum(weights, axis=1, keepdims=True)
    return (dot(weights.astype(BF16), values) / total).astype(BF16)


FACTOR = LANES**-0.5 * math.log2(math.e)


def read_labels(p, recv_ref):
    n = p.devices
    label_block = recv_ref[:, p.row_l : p.row_l + SUB, :].reshape(n * SUB, LANES)
    pick = iota((n, n * SUB), 1) - iota((n, n * SUB), 0) * SUB
    labels = dot(onehot(pick == 0), label_block).astype(BF16)
    busy_labels = dot(onehot(pick == SUB // 2), label_block).astype(BF16)
    return labels, busy_labels


def lane_labels(table, width, lane_of):
    n = table.shape[0]
    total = n * width
    lane = iota((1, total), 1)
    spread = dot(table, onehot(iota((LANES, total), 0) == lane_of(lane & (width - 1))))
    mine = iota((n, total), 0) == (lane >> shift_of(width))
    return jnp.sum(jnp.where(mine, spread, 0.0), axis=0, keepdims=True)


def row_labels(table, width, offset):
    n = table.shape[0]
    total = n * width
    rows = iota((total, n), 0)
    spread = dot(onehot((rows >> shift_of(width)) == iota((total, n), 1)), table)
    lane = (iota((total, LANES), 0) & (width - 1)) + offset
    return jnp.sum(
        jnp.where(iota((total, LANES), 1) == lane, spread, 0.0), axis=1, keepdims=True
    )


def attend_head(p, h, labels, recv_ref, ans_ref):
    n = p.devices
    block = math.gcd(n, max(1, 256 // p.stride))
    key_label = lane_labels(labels, p.stride, lambda within: within + h * p.stride)
    query_label = row_labels(labels, p.stride, h * p.stride)
    row = 3 * h * p.stride
    for start in range(0, n, block):
        size, keys = block * p.stride, (start + block) * p.stride
        first = start * p.stride
        queries = recv_ref[start : start + block, row : row + p.stride, :]
        keys_part = recv_ref[: start + block, row + p.stride : row + 2 * p.stride, :]
        values = recv_ref[: start + block, row + 2 * p.stride : row + 3 * p.stride, :]
        scores = dot_t(queries.reshape(size, LANES), keys_part.reshape(keys, LANES))
        allowed = (query_label[first : first + size] == key_label[:, :keys]) & (
            iota((size, keys), 1) <= iota((size, keys), 0) + first
        )
        out = softmax_rows(scores, allowed, values.reshape(keys, LANES), FACTOR)
        ans_ref[start : start + block, h * p.stride : (h + 1) * p.stride, :] = out.reshape(
            block, p.stride, LANES
        )


def attend_busy(p, me, busy_labels, recv_ref, kv_ref, ans_ref):
    n = p.devices
    mine = lax.rem(me, p.servers)

    def lane_of(within):
        inner = within & (p.qstride - 1)
        return jnp.where(
            inner < p.share, (within >> shift_of(p.qstride)) * p.share + inner, LANES
        )

    key_label = lane_labels(busy_labels, p.extra, lane_of)
    query_label = row_labels(busy_labels, p.qstride, mine * p.share)
    block = math.gcd(n, max(1, 128 // p.qstride))
    for start in range(0, n, block):
        size, keys = block * p.qstride, (start + block) * p.extra
        first = start * p.qstride
        queries = recv_ref[start : start + block, p.row_q : p.row_q + p.qstride, :]
        keys_part = kv_ref[: start + block, :, : p.qstride, :]
        values = kv_ref[: start + block, :, p.qstride :, :]
        scores = dot_t(queries.reshape(size, LANES), keys_part.reshape(keys, LANES))
        rows = iota((size, 1), 0)
        place = (
            ((rows >> shift_of(p.qstride)) + start) * p.extra
            + (rows & (p.qstride - 1))
            + mine * p.qstride
        )
        allowed = (query_label[first : first + size] == key_label[:, :keys]) & (
            iota((size, keys), 1) <= place
        )
        out = softmax_rows(scores, allowed, values.reshape(keys, LANES), FACTOR)
        ans_ref[start : start + block, p.ans_q : p.ans_q + p.qstride, :] = out.reshape(
            block, p.qstride, LANES
        )


def unpack_head(p, h, key_columns, back_ref, out_ref):
    total = p.base + p.extra
    select = onehot(iota((p.tokens, total), 1) == key_columns[:, h : h + 1])
    rows = back_ref[:, h * p.stride : (h + 1) * p.stride, :].reshape(p.base, LANES)
    first = h * p.per_head
    more = back_ref[first : first + p.servers, p.ans_q : p.ans_q + p.qstride, :]
    rows = jnp.concatenate([rows, more.reshape(p.extra, LANES)], axis=0)
    out_ref[:, h * LANES : (h + 1) * LANES] = dot(select, rows).astype(BF16)


def kernel(
    p, groups, members, ids_ref, q_ref, k_ref, v_ref, out_ref,
    send_ref, recv_ref, ans_ref, back_ref, kv_ref, key_ref, base_key_ref,
    send_sem, recv_sem, own_sem,
):
    n = p.devices
    me = lax.axis_index("grp") * members + lax.axis_index("ctx")

    def device(target):
        return (lax.div(target, members), lax.rem(target, members))

    def peer(step):
        hop = lax.rem(step, groups) * members + lax.div(step, groups)
        return lax.rem(me + hop, n)

    barrier = pltpu.get_barrier_semaphore()

    @pl.loop(1, n)
    def _(step):
        pl.semaphore_signal(
            barrier, inc=1, device_id=device(peer(step)), device_id_type=pl.DeviceIdType.MESH
        )

    def start(source, target_ref, row, count, c):
        @pl.loop(1, n)
        def _(step):
            other = peer(step)
            pltpu.make_async_remote_copy(
                src_ref=source.at[other, pl.ds(row, count)],
                dst_ref=target_ref.at[me, pl.ds(row, count)],
                send_sem=send_sem.at[c],
                recv_sem=recv_sem.at[c],
                device_id=device(other),
                device_id_type=pl.DeviceIdType.MESH,
            ).start()

        pltpu.make_async_copy(
            source.at[me, pl.ds(row, count)], target_ref.at[me, pl.ds(row, count)], own_sem.at[c]
        ).start()

    def wait_bytes(ref, row, count, sem):
        part = ref.at[pl.ds(0, n - 1), pl.ds(row, count)]
        pltpu.make_async_copy(part, part, sem).wait()

    def finish(source, target_ref, row, count, c):
        wait_bytes(target_ref, row, count, recv_sem.at[c])
        pltpu.make_async_copy(
            source.at[me, pl.ds(row, count)], target_ref.at[me, pl.ds(row, count)], own_sem.at[c]
        ).wait()

    pack_shared(p, ids_ref, q_ref, k_ref, v_ref, send_ref, key_ref, base_key_ref)
    pl.semaphore_wait(barrier, n - 1)
    start(send_ref, recv_ref, *p.chunks[0], 0)
    for h in range(p.heads):
        pack_head(p, h, q_ref, k_ref, v_ref, send_ref, base_key_ref)
        start(send_ref, recv_ref, *p.chunks[1 + h], 1 + h)

    finish(send_ref, recv_ref, *p.chunks[0], 0)
    mine = lax.rem(me, p.servers)
    shared = recv_ref.at[:, pl.ds(p.row_b, 2 * p.qstride)]
    kv_c = 2 * (p.heads + 1)

    @pl.loop(1, p.servers)
    def _(step):
        other = me - mine + lax.rem(mine + step, p.servers)
        pltpu.make_async_remote_copy(
            src_ref=shared,
            dst_ref=kv_ref.at[:, mine],
            send_sem=send_sem.at[kv_c],
            recv_sem=recv_sem.at[kv_c],
            device_id=device(other),
            device_id_type=pl.DeviceIdType.MESH,
        ).start()

    own = pltpu.make_async_copy(shared, kv_ref.at[:, mine], own_sem.at[kv_c])
    own.start()
    labels, busy_labels = read_labels(p, recv_ref)
    key_columns = jnp.transpose(key_ref[...]).astype(jnp.int32)
    own.wait()
    others = kv_ref.at[:, pl.ds(0, p.servers - 1)]
    pltpu.make_async_copy(others, others, recv_sem.at[kv_c]).wait()
    attend_busy(p, me, busy_labels, recv_ref, kv_ref, ans_ref)
    base_c = p.heads + 1
    start(ans_ref, back_ref, *p.ans_chunks[0], base_c)
    for h in range(p.heads):
        finish(send_ref, recv_ref, *p.chunks[1 + h], 1 + h)
        attend_head(p, h, labels, recv_ref, ans_ref)
        start(ans_ref, back_ref, *p.ans_chunks[1 + h], base_c + 1 + h)
    finish(ans_ref, back_ref, *p.ans_chunks[0], base_c)
    for h in range(p.heads):
        finish(ans_ref, back_ref, *p.ans_chunks[1 + h], base_c + 1 + h)
        unpack_head(p, h, key_columns, back_ref, out_ref)
    for c in range(p.heads + 1):
        wait_bytes(send_ref, *p.chunks[c], send_sem.at[c])
        wait_bytes(ans_ref, *p.ans_chunks[c], send_sem.at[base_c + c])
    pltpu.make_async_copy(others, others, send_sem.at[kv_c]).wait()


VMEM_SPEC = pl.BlockSpec(memory_space=pltpu.VMEM)


def local(query_rows, key_rows, value_rows, cluster_ids):
    groups, members = lax.axis_size("grp"), lax.axis_size("ctx")
    heads, tokens = cluster_ids.shape
    p = Plan(groups * members, heads, tokens)
    count = 2 * (heads + 1) + 1
    return pl.pallas_call(
        functools.partial(kernel, p, groups, members),
        out_shape=jax.ShapeDtypeStruct((tokens, heads * LANES), BF16),
        in_specs=[VMEM_SPEC] * 4,
        out_specs=VMEM_SPEC,
        scratch_shapes=[
            pltpu.VMEM((p.devices, p.rows, LANES), BF16),
            pltpu.VMEM((p.devices, p.rows, LANES), BF16),
            pltpu.VMEM((p.devices, p.ans_rows, LANES), BF16),
            pltpu.VMEM((p.devices, p.ans_rows, LANES), BF16),
            pltpu.VMEM((p.devices, p.servers, 2 * p.qstride, LANES), BF16),
            pltpu.VMEM((up(heads, 8), tokens), F32),
            pltpu.VMEM((up(heads, 8), tokens), jnp.int32),
            pltpu.SemaphoreType.DMA((count,)),
            pltpu.SemaphoreType.DMA((count,)),
            pltpu.SemaphoreType.DMA((count,)),
        ],
        compiler_params=pltpu.CompilerParams(
            collective_id=0, has_side_effects=True, vmem_limit_bytes=60 * 2**20
        ),
    )(cluster_ids, query_rows, key_rows, value_rows)


def solution(mesh):
    return jax.shard_map(
        local,
        mesh=mesh,
        in_specs=(
            P(("grp", "ctx"), None),
            P(("grp", "ctx"), None),
            P(("grp", "ctx"), None),
            P(None, ("grp", "ctx")),
        ),
        out_specs=P(("grp", "ctx"), None),
        check_vma=False,
    )
```

```python
import functools
import math

import jax
import jax.numpy as jnp
from jax import lax
from jax.experimental import pallas as pl
from jax.experimental.pallas import tpu as pltpu
from jax.sharding import PartitionSpec as P

CL_SHIFT = 3
LANES = 128
SUB = 16
NEG_FILL = -1e30
F32 = jnp.float32
BF16 = jnp.bfloat16


def up(value, step):
    return (value + step - 1) // step * step


class Plan:
    def __init__(self, devices, heads, tokens):
        self.devices, self.heads, self.tokens = devices, heads, tokens
        self.cap = tokens // devices
        self.busy = 3 * tokens // devices
        self.stride = up(self.cap, SUB)
        self.per_head = devices // heads
        self.servers = min(self.per_head, max(1, self.busy // 12))
        self.share = -(-self.busy // self.servers)
        self.base = devices * self.stride
        self.qstride = up(self.share + 2, SUB)
        self.extra = self.servers * self.qstride
        self.row_b = heads * 3 * self.stride
        self.row_q = self.row_b + 2 * self.qstride
        self.rows = self.row_q + self.qstride
        self.ans_q = heads * self.stride
        self.ans_rows = self.ans_q + self.qstride
        self.chunks = [(self.row_b, self.rows - self.row_b)]
        self.chunks += [(3 * h * self.stride, 3 * self.stride) for h in range(heads)]
        self.ans_chunks = [(self.ans_q, self.qstride)]
        self.ans_chunks += [(h * self.stride, self.stride) for h in range(heads)]


def iota(shape, dim):
    return lax.broadcasted_iota(jnp.int32, shape, dim)


def dot(a, b):
    return jnp.dot(a, b, preferred_element_type=F32)


def dot_t(a, b):
    return lax.dot_general(a, b, (((1,), (1,)), ((), ())), preferred_element_type=F32)


def onehot(cond):
    return jnp.where(cond, 1.0, 0.0).astype(BF16)


def shift_of(value):
    assert value & (value - 1) == 0
    return value.bit_length() - 1


def pack_shared(p, ids_ref, q_ref, k_ref, v_ref, send_ref, key_ref, base_key_ref, after_first):
    n, t = p.devices, p.tokens
    earlier = onehot(iota((t, t), 0) < iota((t, t), 1))
    key_ref[...] = jnp.zeros(key_ref.shape, F32)
    label_sum = jnp.zeros((n, LANES), F32)
    busy_sum = jnp.zeros((n, LANES), F32)
    query_blocks = []
    for h in range(p.heads):
        ids = ids_ref[h : h + 1, :]
        owner = lax.shift_right_logical(ids, CL_SHIFT)
        label = ((ids & (2**CL_SHIFT - 1)) + 1).astype(F32)
        member = jnp.where(iota((n, t), 0) == owner, 1.0, 0.0)
        rank = dot(member.astype(BF16), earlier)
        slot = jnp.sum(member * rank, axis=0, keepdims=True)
        full = jnp.where(jnp.sum(member, axis=1, keepdims=True) > p.cap, 1.0, 0.0)
        is_busy = jnp.sum(member * full, axis=0, keepdims=True) > 0.5
        share_pos = jnp.floor((slot + 0.5) * (1.0 / p.share))
        key_ref[h : h + 1, :] = jnp.where(
            is_busy,
            p.base + slot + share_pos * (p.qstride - p.share),
            owner.astype(F32) * p.stride + slot,
        )
        slot_i = slot.astype(jnp.int32)
        base_key_ref[h : h + 1, :] = jnp.where(is_busy, -1, owner * p.stride + slot_i)
        if h == 0:
            after_first()
        rank_busy = jnp.where(is_busy, slot_i, -1)
        place = jnp.where(is_busy, -1, h * p.stride + slot_i)
        columns = pl.ds(h * LANES, LANES)
        data = jnp.concatenate([k_ref[:, columns], v_ref[:, columns], q_ref[:, columns]], axis=1)
        rows = iota((p.extra, t), 0)
        within = rows & (p.qstride - 1)
        wanted = lax.shift_right_logical(rows, shift_of(p.qstride)) * p.share + within
        wanted = jnp.where(within < p.share, wanted, -2)
        exact = dot(onehot(wanted == rank_busy), data)
        moved = exact.astype(BF16)
        first = h * p.per_head
        for part in range(2):
            row = p.row_b + part * p.qstride
            send_ref[first : first + p.servers, row : row + p.qstride, :] = moved[
                :, part * LANES : (part + 1) * LANES
            ].reshape(p.servers, p.qstride, LANES)
        query_blocks.append(exact[:, 2 * LANES :])
        spare = p.per_head - p.servers
        if spare > 0:
            send_ref[
                first + p.servers : first + p.per_head, p.row_b : p.row_q, :
            ] = jnp.zeros((spare, 2 * p.qstride, LANES), BF16)
            query_blocks.append(jnp.zeros((spare * p.qstride, LANES), F32))
        spot = onehot(iota((LANES, t), 0) == place)
        label_sum += dot_t((member * label).astype(BF16), spot)
        spot = onehot(iota((LANES, t), 0) == rank_busy)
        line = dot_t(jnp.broadcast_to(label, (8, t)).astype(BF16), spot)[:1]
        mine = lax.shift_right_logical(iota((n, LANES), 0), shift_of(p.per_head)) == h
        busy_sum += jnp.where(mine, jnp.broadcast_to(line, (n, LANES)), 0.0)
    place = iota((n * p.qstride, n), 0) - iota((n * p.qstride, n), 1) * p.qstride
    both = dot(onehot(place == p.share), label_sum.astype(BF16)) + dot(
        onehot(place == p.share + 1), busy_sum.astype(BF16)
    )
    both += jnp.concatenate(query_blocks, axis=0)
    send_ref[:, p.row_q : p.row_q + p.qstride, :] = both.astype(BF16).reshape(
        n, p.qstride, LANES
    )


def pack_head(p, h, q_ref, k_ref, v_ref, send_ref, base_key_ref):
    columns = pl.ds(h * LANES, LANES)
    data = jnp.concatenate([q_ref[:, columns], k_ref[:, columns], v_ref[:, columns]], axis=1)
    select = onehot(iota((p.base, p.tokens), 0) == base_key_ref[h : h + 1, :])
    moved = dot(select, data).astype(BF16)
    for part in range(3):
        row = (3 * h + part) * p.stride
        send_ref[:, row : row + p.stride, :] = moved[
            :, part * LANES : (part + 1) * LANES
        ].reshape(p.devices, p.stride, LANES)


def softmax_rows(scores, allowed, values, factor):
    masked = jnp.where(allowed, scores, NEG_FILL)
    top = jnp.max(masked, axis=1, keepdims=True)
    weights = jnp.exp2((masked - top) * factor)
    total = jnp.sum(weights, axis=1, keepdims=True)
    return (dot(weights.astype(BF16), values) / total).astype(BF16)


FACTOR = LANES**-0.5 * math.log2(math.e)


def read_labels(p, recv_ref):
    n = p.devices
    total = n * p.qstride
    label_block = recv_ref[:, p.row_q : p.row_q + p.qstride, :].reshape(total, LANES)
    pick = iota((n, total), 1) - iota((n, total), 0) * p.qstride
    labels = dot(onehot(pick == p.share), label_block).astype(BF16)
    busy_labels = dot(onehot(pick == p.share + 1), label_block).astype(BF16)
    return labels, busy_labels


def lane_labels(table, width, lane_of):
    n = table.shape[0]
    total = n * width
    lane = iota((1, total), 1)
    spread = dot(table, onehot(iota((LANES, total), 0) == lane_of(lane & (width - 1))))
    mine = iota((n, total), 0) == (lane >> shift_of(width))
    return jnp.sum(jnp.where(mine, spread, 0.0), axis=0, keepdims=True)


def row_labels(table, width, offset):
    n = table.shape[0]
    total = n * width
    rows = iota((total, n), 0)
    spread = dot(onehot((rows >> shift_of(width)) == iota((total, n), 1)), table)
    lane = (iota((total, LANES), 0) & (width - 1)) + offset
    return jnp.sum(
        jnp.where(iota((total, LANES), 1) == lane, spread, 0.0), axis=1, keepdims=True
    )


def attend_head(p, h, labels, recv_ref, ans_ref):
    n = p.devices
    block = math.gcd(n, max(1, 256 // p.stride))
    key_label = lane_labels(labels, p.stride, lambda within: within + h * p.stride)
    query_label = row_labels(labels, p.stride, h * p.stride)
    row = 3 * h * p.stride
    for start in range(0, n, block):
        size, keys = block * p.stride, (start + block) * p.stride
        first = start * p.stride
        queries = recv_ref[start : start + block, row : row + p.stride, :]
        keys_part = recv_ref[: start + block, row + p.stride : row + 2 * p.stride, :]
        values = recv_ref[: start + block, row + 2 * p.stride : row + 3 * p.stride, :]
        scores = dot_t(queries.reshape(size, LANES), keys_part.reshape(keys, LANES))
        allowed = (query_label[first : first + size] == key_label[:, :keys]) & (
            iota((size, keys), 1) <= iota((size, keys), 0) + first
        )
        out = softmax_rows(scores, allowed, values.reshape(keys, LANES), FACTOR)
        ans_ref[start : start + block, h * p.stride : (h + 1) * p.stride, :] = out.reshape(
            block, p.stride, LANES
        )


def attend_busy(p, me, busy_labels, recv_ref, kv_ref, ans_ref):
    n = p.devices
    mine = lax.rem(me, p.servers)

    def lane_of(within):
        inner = within & (p.qstride - 1)
        return jnp.where(
            inner < p.share, (within >> shift_of(p.qstride)) * p.share + inner, LANES
        )

    key_label = lane_labels(busy_labels, p.extra, lane_of)
    query_label = row_labels(busy_labels, p.qstride, mine * p.share)
    block = math.gcd(n, max(1, 128 // p.qstride))
    for start in range(0, n, block):
        size, keys = block * p.qstride, (start + block) * p.extra
        first = start * p.qstride
        queries = recv_ref[start : start + block, p.row_q : p.row_q + p.qstride, :]
        keys_part = kv_ref[: start + block, :, : p.qstride, :]
        values = kv_ref[: start + block, :, p.qstride :, :]
        scores = dot_t(queries.reshape(size, LANES), keys_part.reshape(keys, LANES))
        rows = iota((size, 1), 0)
        place = (
            ((rows >> shift_of(p.qstride)) + start) * p.extra
            + (rows & (p.qstride - 1))
            + mine * p.qstride
        )
        allowed = (query_label[first : first + size] == key_label[:, :keys]) & (
            iota((size, keys), 1) <= place
        )
        out = softmax_rows(scores, allowed, values.reshape(keys, LANES), FACTOR)
        ans_ref[start : start + block, p.ans_q : p.ans_q + p.qstride, :] = out.reshape(
            block, p.qstride, LANES
        )


def unpack_head(p, h, key_columns, back_ref, out_ref):
    total = p.base + p.extra
    select = onehot(iota((p.tokens, total), 1) == key_columns[:, h : h + 1])
    rows = back_ref[:, h * p.stride : (h + 1) * p.stride, :].reshape(p.base, LANES)
    first = h * p.per_head
    more = back_ref[first : first + p.servers, p.ans_q : p.ans_q + p.qstride, :]
    rows = jnp.concatenate([rows, more.reshape(p.extra, LANES)], axis=0)
    out_ref[:, h * LANES : (h + 1) * LANES] = dot(select, rows).astype(BF16)


def kernel(
    p, groups, members, ids_ref, q_ref, k_ref, v_ref, out_ref,
    send_ref, recv_ref, ans_ref, back_ref, kv_ref, key_ref, base_key_ref,
    send_sem, recv_sem, own_sem,
):
    n = p.devices
    me = lax.axis_index("grp") * members + lax.axis_index("ctx")

    def device(target):
        return (lax.div(target, members), lax.rem(target, members))

    def peer(step):
        hop = lax.rem(step, groups) * members + lax.div(step, groups)
        return lax.rem(me + hop, n)

    barrier = pltpu.get_barrier_semaphore()

    @pl.loop(1, n)
    def _(step):
        pl.semaphore_signal(
            barrier, inc=1, device_id=device(peer(step)), device_id_type=pl.DeviceIdType.MESH
        )

    def start(source, target_ref, row, count, c):
        @pl.loop(1, n)
        def _(step):
            other = peer(step)
            pltpu.make_async_remote_copy(
                src_ref=source.at[other, pl.ds(row, count)],
                dst_ref=target_ref.at[me, pl.ds(row, count)],
                send_sem=send_sem.at[c],
                recv_sem=recv_sem.at[c],
                device_id=device(other),
                device_id_type=pl.DeviceIdType.MESH,
            ).start()

        pltpu.make_async_copy(
            source.at[me, pl.ds(row, count)], target_ref.at[me, pl.ds(row, count)], own_sem.at[c]
        ).start()

    def wait_bytes(ref, row, count, sem):
        part = ref.at[pl.ds(0, n - 1), pl.ds(row, count)]
        pltpu.make_async_copy(part, part, sem).wait()

    def finish(source, target_ref, row, count, c):
        wait_bytes(target_ref, row, count, recv_sem.at[c])
        pltpu.make_async_copy(
            source.at[me, pl.ds(row, count)], target_ref.at[me, pl.ds(row, count)], own_sem.at[c]
        ).wait()

    def after_first():
        pack_head(p, 0, q_ref, k_ref, v_ref, send_ref, base_key_ref)
        pl.semaphore_wait(barrier, n - 1)
        start(send_ref, recv_ref, *p.chunks[1], 1)

    pack_shared(
        p, ids_ref, q_ref, k_ref, v_ref, send_ref, key_ref, base_key_ref, after_first
    )
    start(send_ref, recv_ref, *p.chunks[0], 0)
    for h in range(1, p.heads):
        pack_head(p, h, q_ref, k_ref, v_ref, send_ref, base_key_ref)
        start(send_ref, recv_ref, *p.chunks[1 + h], 1 + h)

    finish(send_ref, recv_ref, *p.chunks[0], 0)
    mine = lax.rem(me, p.servers)
    shared = recv_ref.at[:, pl.ds(p.row_b, 2 * p.qstride)]
    kv_c = 2 * (p.heads + 1)

    @pl.loop(1, p.servers)
    def _(step):
        other = me - mine + lax.rem(mine + step, p.servers)
        pltpu.make_async_remote_copy(
            src_ref=shared,
            dst_ref=kv_ref.at[:, mine],
            send_sem=send_sem.at[kv_c],
            recv_sem=recv_sem.at[kv_c],
            device_id=device(other),
            device_id_type=pl.DeviceIdType.MESH,
        ).start()

    own = pltpu.make_async_copy(shared, kv_ref.at[:, mine], own_sem.at[kv_c])
    own.start()
    labels, busy_labels = read_labels(p, recv_ref)
    key_columns = jnp.transpose(key_ref[...]).astype(jnp.int32)
    others = kv_ref.at[:, pl.ds(0, p.servers - 1)]
    base_c = p.heads + 1
    for h in range(p.heads):
        if h == p.heads - 1:
            own.wait()
            pltpu.make_async_copy(others, others, recv_sem.at[kv_c]).wait()
            attend_busy(p, me, busy_labels, recv_ref, kv_ref, ans_ref)
            start(ans_ref, back_ref, *p.ans_chunks[0], base_c)
        finish(send_ref, recv_ref, *p.chunks[1 + h], 1 + h)
        attend_head(p, h, labels, recv_ref, ans_ref)
        start(ans_ref, back_ref, *p.ans_chunks[1 + h], base_c + 1 + h)
    finish(ans_ref, back_ref, *p.ans_chunks[0], base_c)
    for h in range(p.heads):
        finish(ans_ref, back_ref, *p.ans_chunks[1 + h], base_c + 1 + h)
        unpack_head(p, h, key_columns, back_ref, out_ref)
    for c in range(p.heads + 1):
        wait_bytes(send_ref, *p.chunks[c], send_sem.at[c])
        wait_bytes(ans_ref, *p.ans_chunks[c], send_sem.at[base_c + c])
    pltpu.make_async_copy(others, others, send_sem.at[kv_c]).wait()


VMEM_SPEC = pl.BlockSpec(memory_space=pltpu.VMEM)


def local(query_rows, key_rows, value_rows, cluster_ids):
    groups, members = lax.axis_size("grp"), lax.axis_size("ctx")
    heads, tokens = cluster_ids.shape
    p = Plan(groups * members, heads, tokens)
    count = 2 * (heads + 1) + 1
    return pl.pallas_call(
        functools.partial(kernel, p, groups, members),
        out_shape=jax.ShapeDtypeStruct((tokens, heads * LANES), BF16),
        in_specs=[VMEM_SPEC] * 4,
        out_specs=VMEM_SPEC,
        scratch_shapes=[
            pltpu.VMEM((p.devices, p.rows, LANES), BF16),
            pltpu.VMEM((p.devices, p.rows, LANES), BF16),
            pltpu.VMEM((p.devices, p.ans_rows, LANES), BF16),
            pltpu.VMEM((p.devices, p.ans_rows, LANES), BF16),
            pltpu.VMEM((p.devices, p.servers, 2 * p.qstride, LANES), BF16),
            pltpu.VMEM((up(heads, 8), tokens), F32),
            pltpu.VMEM((up(heads, 8), tokens), jnp.int32),
            pltpu.SemaphoreType.DMA((count,)),
            pltpu.SemaphoreType.DMA((count,)),
            pltpu.SemaphoreType.DMA((count,)),
        ],
        compiler_params=pltpu.CompilerParams(
            collective_id=0, has_side_effects=True, vmem_limit_bytes=60 * 2**20
        ),
    )(cluster_ids, query_rows, key_rows, value_rows)


def solution(mesh):
    return jax.shard_map(
        local,
        mesh=mesh,
        in_specs=(
            P(("grp", "ctx"), None),
            P(("grp", "ctx"), None),
            P(("grp", "ctx"), None),
            P(None, ("grp", "ctx")),
        ),
        out_specs=P(("grp", "ctx"), None),
        check_vma=False,
    )
```
